512 devices in a mesh: grp: 16 (over y_hi, x, core), ops: 32 (over y_lo, z).
Axes of the slice: x: 4, y: 4 (y_hi: 2, y_lo: 2; y = y_hi * 2 + y_lo), z: 16, core: 2. Of those that a mesh axis runs over, the one named last changes fastest.
Arguments:
- psi: bfloat16 [112, 384, 384], P('grp', 'ops'), may hold values from -6 to 6
- left_ops: bfloat16 [112, 32, 384, 384], P('grp', 'ops'), may hold values from -1 to 2
- right_ops: bfloat16 [112, 32, 384, 384], P('grp', 'ops'), may hold values from -1 to 2
- right_group: int32 [112, 1], replicated, may hold values from 0 to 15; in each aligned block of 7 rows (0 to 6, 7 to 13, ...) no two rows name the same one
- right_slot: int32 [112], replicated, may hold values from 0 to 6
- precond_diag: float32 [112, 384, 384], P('grp', 'ops'), may hold values from 0.25 to 8
Outputs:
- sigma: float32 [112, 384, 384], P('grp', 'ops')
- correction: float32 [112, 384, 384], P('grp', 'ops')
The draws below stay inside these ranges and needn't reach their ends.
Inputs may be any that keep to these rules, and one draw needn't show every extreme that they name: In the 7 sectors of one group, at most 1 have their right_group equal to any one group; some group reaches 1.
All inputs are finite; a program needn't handle non-finite values.
Results may differ from the reference program's by a relative error of at most 0.0006.
The reference program's roundings to bfloat16 on the way (of `image`) count: a program that leaves them out, or rounds other values in their place, can miss the bound.
Values may be sent and summed in bfloat16 or wider, within the bound.
No kernel may reach another device: no remote copies, remote signals or barrier semaphores. Data moves between devices by JAX's collectives and lax.ppermute only.
A program may use at most 64 MiB of HBM per device.

```python
import math
import jax
import jax.numpy as jnp
import numpy as np
from jax import lax

SEC = 384
SPG = 7
NSEC = 112
K = 32
CAP = 1
N_GRP = 16


def operator_blocks(key):
    noise = jax.random.normal(key, (NSEC, K, SEC, SEC), jnp.float32)
    return jnp.eye(SEC, dtype=jnp.float32) + 0.5 * noise / math.sqrt(SEC)


def draw_left_ops(key, part):
    return operator_blocks(jax.random.fold_in(key, 11)).astype(jnp.bfloat16)


def draw_right_ops(key, part):
    return (operator_blocks(jax.random.fold_in(key, 23)) / K).astype(jnp.bfloat16)


def plant(result, own_key, least, high):
    spot = [jax.random.randint(jax.random.fold_in(own_key, axis), (), 0, length) for axis, length in enumerate(result.shape)]
    main_axis = result.shape.index(max(result.shape))
    beside = spot[:main_axis] + [(spot[main_axis] + 1) % result.shape[main_axis]] + spot[main_axis + 1:]
    return result.at[tuple(spot)].set(least).at[tuple(beside)].set(high)


def level_of(stream_key, dims, shards, low, largest):
    gain = 1.0
    for axis_at, parts in shards:
        draws = jax.random.uniform(jax.random.fold_in(jax.random.fold_in(stream_key, 6), axis_at), (parts,), jnp.float32, low / len(shards), largest / len(shards))
        gain = gain * jnp.repeat(jnp.exp(draws), dims[axis_at] // parts).reshape((-1,) + (1,) * (len(dims) - 1 - axis_at))
    return gain


def assign_block(key, own, number, rows, amount, top, most, lean):
    order = jax.random.permutation(key, amount)
    packed, ordinary = portions_of(amount, rows * top, most, lean, True), portions_of(amount, rows * top, most, lean, False)
    places = jnp.arange(amount)

    def named(sizes, turn):
        used = int((sizes > 0).sum())
        fixed = max(1, used // 4)
        moved = fixed + (places - fixed + turn * (used - fixed)) % max(1, amount - fixed)
        return jnp.zeros((amount,), jnp.int32).at[order[jnp.where(places < fixed, places, moved)]].set(jnp.asarray(sizes, jnp.int32))

    sizes = jnp.where(number % 4 == 0, named(packed, number // 4), named(ordinary, number - number // 4 - 1))
    mixed = jax.random.permutation(jax.random.fold_in(own, 3), amount)
    source_of, taker = mixed[0:amount // 2 * 2:2], mixed[1:amount // 2 * 2:2]
    margin = jnp.minimum(sizes[source_of] - 1, most - sizes[taker]) // 2
    margin = jnp.where((source_of == order[0]) | (taker == order[0]) | (sizes[taker] == 0), 0, jnp.maximum(margin, 0))
    moved = jax.random.randint(jax.random.fold_in(own, 4), (amount // 2,), 0, 1 << 20) % (margin + 1)
    sizes = sizes.at[source_of].add(-moved).at[taker].add(moved)
    items = jnp.searchsorted(jnp.cumsum(sizes), jnp.arange(rows * top), side="right").astype(jnp.int32)
    table = items.reshape(top, rows).T
    table = table[jax.random.permutation(jax.random.fold_in(own, 1), rows)]
    turn = jax.random.randint(jax.random.fold_in(own, 2), (rows, 1), 0, top)
    return jnp.take_along_axis(table, (jnp.arange(top)[None, :] + turn) % top, axis=1)


def portions_of(number_of, total, bound, slope, full):
    portions = [(1 << 20) // math.isqrt(grade ** slope) + 1 for grade in range(1, number_of + 1)]
    largest = bound if full else min(bound, max(-(-total // number_of), total * portions[0] // sum(portions)))
    least = 1 if total - largest >= number_of - 1 else 0
    holding, surplus = [largest] + [least] * (number_of - 1), total - largest - least * (number_of - 1)
    while surplus > 0:
        candidates = [i for i in range(1, number_of) if holding[i] < largest] or [i for i in range(1, number_of) if holding[i] < bound]
        pool, left = sum([portions[i] for i in candidates]), surplus
        for i in candidates:
            extra = min(bound - holding[i], max(1, left * portions[i] // pool), surplus)
            holding[i] = holding[i] + extra
            surplus = surplus - extra
    return np.array(holding)


def gaussian(stream_key, extent, spread, most, cuts=(), kind=jnp.bfloat16):
    factor_of = level_of(stream_key, extent, cuts, -0.22, 0.18) if cuts else 1.0
    drawn = jax.random.normal(stream_key, extent, jnp.float32) * spread * factor_of
    return jnp.minimum(jnp.maximum(drawn, -most), most).astype(kind)


def setup_inputs(seed: int = 0) -> dict:
    key_list = jax.random.split(jax.random.key(seed), 7)
    psi = gaussian(key_list[0], (NSEC, SEC, SEC), 1.0, 6.0, ((0, 16), (1, 32)))
    left_ops = draw_left_ops(jax.random.fold_in(key_list[6], 71), 0)
    right_ops = draw_right_ops(jax.random.fold_in(key_list[6], 71), 0)
    right_group_keys = jax.random.split(jax.random.fold_in(key_list[3], 1), NSEC // SPG)
    right_group_turns = jax.random.permutation(jax.random.fold_in(key_list[3], 3), NSEC // SPG)
    right_group = jax.vmap(lambda own, number: assign_block(jax.random.fold_in(key_list[3], 2), own, number, SPG, N_GRP, 1, CAP, 2))(right_group_keys, right_group_turns).reshape((NSEC, 1))
    right_slot = plant(jax.random.randint(key_list[4], (NSEC,), 0, SPG), jax.random.fold_in(key_list[4], 1), 0, SPG - 1).astype(jnp.int32)
    precond_diag = jnp.clip(jnp.exp(math.log(8.0) - 3.465736 * jax.random.uniform(key_list[5], (NSEC, SEC, SEC), jnp.float32) ** level_of(key_list[5], (NSEC, SEC, SEC), ((0, 16), (1, 32)), -0.2, 0.2)), 0.25, 8.0)
    return {"psi": psi, "left_ops": left_ops, "right_ops": right_ops, "right_group": right_group, "right_slot": right_slot, "precond_diag": precond_diag}


def reference(psi, left_ops, right_ops, right_group, right_slot, precond_diag):
    partner = (right_group[:, 0] * SPG + right_slot).astype(jnp.int32)

    def sector(index):
        block = psi[index]
        lefts = left_ops[index]
        rights = right_ops[partner[index]]

        def term(total, pair):
            left, right = pair
            image = jnp.dot(block, right.T, preferred_element_type=jnp.float32).astype(jnp.bfloat16)
            return total + jnp.dot(left, image, preferred_element_type=jnp.float32), None

        total, _ = lax.scan(term, jnp.zeros((SEC, SEC), jnp.float32), (lefts, rights))
        return total

    sigma = lax.map(sector, jnp.arange(NSEC, dtype=jnp.int32))
    wave = psi.astype(jnp.float32)
    theta = jnp.sum(wave * sigma) / jnp.sum(wave * wave)
    gap = precond_diag - theta
    correction = (sigma - theta * wave) * gap / (gap * gap + 1.0)
    return sigma, correction
```

```python
import jax
import jax.numpy as jnp
from jax import lax
from jax.experimental import pallas as pl
from jax.experimental.pallas import tpu as pltpu
from jax.sharding import Mesh
from jax.sharding import PartitionSpec as P

GRP = ("yh", "x", "c")
OPS = ("yl", "z")
LANES = 128


def pick_kernel(groups_ref, slots_ref, me_ref, right_ref, out_ref):
    out_ref[...] = right_ref[...]


def outgoing_blocks(groups, slots, me, rights, n_groups):
    spg, rows, cols = rights.shape

    def source(g, groups_ref, slots_ref, me_ref):
        slot = 0
        for j in range(spg):
            named = groups_ref[g * spg + j] == me_ref[0]
            slot = jnp.where(named, slots_ref[g * spg + j], slot)
        return slot, 0, 0

    return pl.pallas_call(
        pick_kernel,
        grid_spec=pltpu.PrefetchScalarGridSpec(
            num_scalar_prefetch=3,
            grid=(n_groups,),
            in_specs=[pl.BlockSpec((1, rows, cols), source)],
            out_specs=pl.BlockSpec((1, rows, cols), lambda g, *_: (g, 0, 0)),
        ),
        out_shape=jax.ShapeDtypeStruct((n_groups, rows, cols), rights.dtype),
        name="pick",
    )(groups, slots, me, rights)


def sigma_kernel(shape, groups_ref, me_ref, half_ref, norm_ref, own_ref, other_ref, left_ref, right_ref, out_ref, psi_ref, part_ref, corr_ref):
    n_z, n_y, part, chunks, extra, stride = shape
    j = pl.program_id(0)
    spg = pl.num_programs(0)
    half = own_ref.shape[1]
    psi_ref[pl.ds(pl.multiple_of(half_ref[0] * half, half), half), :] = own_ref[0]
    psi_ref[pl.ds(pl.multiple_of((1 - half_ref[0]) * half, half), half), :] = other_ref[0]
    psi = psi_ref[...]
    image = lax.dot_general(psi, right_ref[0], (((1,), (1,)), ((), ())), preferred_element_type=jnp.float32)
    total = jnp.dot(left_ref[0], image.astype(jnp.bfloat16), preferred_element_type=jnp.float32)
    weighted = psi.astype(jnp.float32) * total
    folded = jnp.sum(weighted.reshape(-1, 8, weighted.shape[1]), axis=0)
    corr = sum(folded[:, c * LANES : (c + 1) * LANES] for c in range(chunks))

    @pl.when(j == 0)
    def _():
        corr_ref[...] = corr

    @pl.when(j > 0)
    def _():
        corr_ref[...] += corr

    for c in range(chunks):
        part_ref[c] = total[:, c * LANES : (c + 1) * LANES]
    width = chunks * part
    for y in range(n_y):
        for z in range(n_z):
            for c in range(chunks):
                rows = part_ref[c, pl.ds(y * half + z * part, part), :]
                out_ref[pl.ds(z * stride + y * spg_rows(shape) + c * part + j * width, part), :] = rows

    @pl.when(j == spg - 1)
    def _():
        top = jnp.sum(corr_ref[...], axis=0, keepdims=True)
        below = jnp.zeros((extra - 2, LANES), jnp.float32)
        tail = jnp.concatenate([top, norm_ref[...], below], axis=0)
        for z in range(n_z):
            out_ref[pl.ds((z + 1) * stride - extra, extra), :] = tail


def spg_rows(shape):
    n_z, n_y, part, chunks, extra, stride = shape
    return (stride - extra) // n_y


def partial_sums(groups, me, half, norm, own, other, lefts, incoming, shape):
    spg, rows, cols = lefts.shape
    n_z, n_y, part, chunks, extra, stride = shape

    def kernel(*refs):
        sigma_kernel(shape, *refs)

    sector = lambda j, *_: (j, 0, 0)
    return pl.pallas_call(
        kernel,
        grid_spec=pltpu.PrefetchScalarGridSpec(
            num_scalar_prefetch=3,
            grid=(spg,),
            in_specs=[
                pl.BlockSpec((1, LANES), lambda j, *_: (0, 0)),
                pl.BlockSpec((1, rows // n_y, cols), sector),
                pl.BlockSpec((1, rows // n_y, cols), sector),
                pl.BlockSpec((1, rows, cols), sector),
                pl.BlockSpec((1, rows, cols), lambda j, g, m, h: (g[m[0] * spg + j], 0, 0)),
            ],
            out_specs=pl.BlockSpec((n_z * stride, LANES), lambda j, *_: (0, 0)),
            scratch_shapes=[
                pltpu.VMEM((rows, cols), jnp.bfloat16),
                pltpu.VMEM((chunks, rows, LANES), jnp.float32),
                pltpu.VMEM((8, LANES), jnp.float32),
            ],
        ),
        out_shape=jax.ShapeDtypeStruct((n_z * stride, LANES), jnp.float32),
        name="partial",
    )(groups, me, half, norm, own, other, lefts, incoming)


def shards(psi, left_ops, right_ops, right_group, right_slot, precond_diag):
    n_groups, n_z, n_y = lax.axis_size(GRP), lax.axis_size("z"), lax.axis_size("yl")
    spg, part, cols = psi.shape
    chunks = cols // LANES
    me = lax.axis_index(GRP).astype(jnp.int32).reshape(1)
    half = lax.axis_index("yl").astype(jnp.int32)
    groups = right_group.reshape(-1)

    mine = jnp.transpose(psi, (1, 0, 2))
    theirs = lax.ppermute(mine, "yl", [(0, 1), (1, 0)])
    outgoing = outgoing_blocks(groups, right_slot, me, right_ops[:, 0], n_groups)
    incoming = lax.all_to_all(outgoing, GRP, split_axis=0, concat_axis=0, tiled=True)
    own = lax.all_gather(mine, "z", axis=0, tiled=True)
    other = lax.all_gather(theirs, "z", axis=0, tiled=True)
    own = jnp.transpose(own, (1, 0, 2))
    other = jnp.transpose(other, (1, 0, 2))

    wave = psi.astype(jnp.float32)
    norm = jnp.sum(jnp.sum(wave * wave, axis=(0, 1)).reshape(chunks, 1, LANES), axis=0)
    block = spg * part * chunks
    extra = 4
    stride = n_y * block + extra
    shape = (n_z, n_y, part, chunks, extra, stride)
    partials = partial_sums(groups, me, half.reshape(1), norm, own, other, left_ops[:, 0], incoming, shape)

    summed = lax.psum_scatter(partials, "z", scatter_dimension=0, tiled=True)
    summed = lax.optimization_barrier(summed)
    kept = lax.dynamic_slice_in_dim(summed, half * block, block, 0)
    given = lax.dynamic_slice_in_dim(summed, (1 - half) * block, block, 0)
    taken = lax.ppermute(given, "yl", [(0, 1), (1, 0)])
    scalars = summed[n_y * block : n_y * block + 2].reshape(1, 2, LANES)
    spread = ("yh", "x", "c", "yl")
    copies = jnp.broadcast_to(scalars, (lax.axis_size(spread), 2, LANES))
    both = jnp.sum(lax.all_to_all(copies, spread, split_axis=0, concat_axis=0, tiled=True), axis=(0, 2))
    theta = both[0] / both[1]
    sigma = (kept + taken).reshape(spg, chunks, part, LANES).transpose(0, 2, 1, 3).reshape(spg, part, cols)
    gap = precond_diag - theta
    correction = (sigma - theta * wave) * gap / (gap * gap + 1.0)
    return (sigma, correction)


def solution(mesh):
    split = Mesh(mesh.devices.reshape(2, 4, 2, 2, 16), GRP + OPS)
    return jax.shard_map(
        shards,
        mesh=split,
        in_specs=(
            P(GRP, OPS, None),
            P(GRP, OPS, None, None),
            P(GRP, OPS, None, None),
            P(),
            P(),
            P(GRP, OPS, None),
        ),
        out_specs=(P(GRP, OPS, None), P(GRP, OPS, None)),
        check_vma=False,
    )
```

```python
import jax
import jax.numpy as jnp
from jax import lax
from jax.experimental import pallas as pl
from jax.experimental.pallas import tpu as pltpu
from jax.sharding import Mesh
from jax.sharding import PartitionSpec as P

GRP = ("yh", "x", "c")
OPS = ("yl", "z")
LANES = 128


def pick_kernel(groups_ref, slots_ref, me_ref, right_ref, out_ref, held_ref, in_sems, out_sems):
    spg, n_groups = held_ref.shape[0], out_ref.shape[0]
    loads = [pltpu.make_async_copy(right_ref.at[j], held_ref.at[j], in_sems.at[j]) for j in range(spg)]
    for load in loads:
        load.start()
    slots = []
    for g in range(n_groups):
        slot = jnp.int32(0)
        for j in range(spg):
            slot = jnp.where(groups_ref[g * spg + j] == me_ref[0], slots_ref[g * spg + j], slot)
        slots.append(slot)
    for load in loads:
        load.wait()
    stores = [pltpu.make_async_copy(held_ref.at[slots[g]], out_ref.at[g], out_sems.at[g]) for g in range(n_groups)]
    for store in stores:
        store.start()
    for store in stores:
        store.wait()


def outgoing_blocks(groups, slots, me, rights, n_groups):
    spg, rows, cols = rights.shape
    scalars = pl.BlockSpec(memory_space=pltpu.SMEM)
    return pl.pallas_call(
        pick_kernel,
        in_specs=[scalars, scalars, scalars, pl.BlockSpec(memory_space=pl.ANY)],
        out_specs=pl.BlockSpec(memory_space=pl.ANY),
        out_shape=jax.ShapeDtypeStruct((n_groups, rows, cols), rights.dtype),
        scratch_shapes=[
            pltpu.VMEM((spg, rows, cols), rights.dtype),
            pltpu.SemaphoreType.DMA((spg,)),
            pltpu.SemaphoreType.DMA((n_groups,)),
        ],
        name="pick",
    )(groups, slots, me, rights)


def sigma_kernel(shape, groups_ref, me_ref, half_ref, norm_ref, own_ref, other_ref, left_ref, right_ref, out_ref, psi_ref, part_ref, corr_ref):
    n_z, n_y, part, chunks, extra, stride = shape
    j = pl.program_id(0)
    spg = pl.num_programs(0)
    half = own_ref.shape[1]
    psi_ref[pl.ds(pl.multiple_of(half_ref[0] * half, half), half), :] = own_ref[0]
    psi_ref[pl.ds(pl.multiple_of((1 - half_ref[0]) * half, half), half), :] = other_ref[0]
    psi = psi_ref[...]
    image = lax.dot_general(psi, right_ref[0], (((1,), (1,)), ((), ())), preferred_element_type=jnp.float32)
    total = jnp.dot(left_ref[0], image.astype(jnp.bfloat16), preferred_element_type=jnp.float32)
    weighted = psi.astype(jnp.float32) * total
    folded = jnp.sum(weighted.reshape(-1, 8, weighted.shape[1]), axis=0)
    corr = sum(folded[:, c * LANES : (c + 1) * LANES] for c in range(chunks))

    @pl.when(j == 0)
    def _():
        corr_ref[...] = corr

    @pl.when(j > 0)
    def _():
        corr_ref[...] += corr

    for c in range(chunks):
        part_ref[c] = total[:, c * LANES : (c + 1) * LANES]
    width = chunks * part
    for y in range(n_y):
        for z in range(n_z):
            for c in range(chunks):
                rows = part_ref[c, pl.ds(y * half + z * part, part), :]
                out_ref[pl.ds(z * stride + y * spg_rows(shape) + c * part + j * width, part), :] = rows

    @pl.when(j == spg - 1)
    def _():
        top = jnp.sum(corr_ref[...], axis=0, keepdims=True)
        below = jnp.zeros((extra - 2, LANES), jnp.float32)
        tail = jnp.concatenate([top, norm_ref[...], below], axis=0)
        for z in range(n_z):
            out_ref[pl.ds((z + 1) * stride - extra, extra), :] = tail


def spg_rows(shape):
    _, n_y, _, _, extra, stride = shape
    return (stride - extra) // n_y


def partial_sums(groups, me, half, norm, own, other, lefts, incoming, shape):
    spg, rows, cols = lefts.shape
    n_z, n_y, _, chunks, _, stride = shape

    def kernel(*refs):
        sigma_kernel(shape, *refs)

    sector = lambda j, *_: (j, 0, 0)
    return pl.pallas_call(
        kernel,
        grid_spec=pltpu.PrefetchScalarGridSpec(
            num_scalar_prefetch=3,
            grid=(spg,),
            in_specs=[
                pl.BlockSpec((1, LANES), lambda j, *_: (0, 0)),
                pl.BlockSpec((1, rows // n_y, cols), sector),
                pl.BlockSpec((1, rows // n_y, cols), sector),
                pl.BlockSpec((1, rows, cols), sector),
                pl.BlockSpec((1, rows, cols), lambda j, g, m, h: (g[m[0] * spg + j], 0, 0)),
            ],
            out_specs=pl.BlockSpec((n_z * stride, LANES), lambda j, *_: (0, 0)),
            scratch_shapes=[
                pltpu.VMEM((rows, cols), jnp.bfloat16),
                pltpu.VMEM((chunks, rows, LANES), jnp.float32),
                pltpu.VMEM((8, LANES), jnp.float32),
            ],
        ),
        out_shape=jax.ShapeDtypeStruct((n_z * stride, LANES), jnp.float32),
        name="partial",
    )(groups, me, half, norm, own, other, lefts, incoming)


def step(psi, left_ops, right_ops, right_group, right_slot, precond_diag):
    n_groups, n_z, n_y = lax.axis_size(GRP), lax.axis_size("z"), lax.axis_size("yl")
    spg, part, cols = psi.shape
    chunks = cols // LANES
    me = lax.axis_index(GRP).astype(jnp.int32).reshape(1)
    half = lax.axis_index("yl").astype(jnp.int32)
    groups = right_group.reshape(-1)

    mine = jnp.transpose(psi, (1, 0, 2))
    outgoing = outgoing_blocks(groups, right_slot, me, right_ops[:, 0], n_groups)
    incoming = lax.all_to_all(outgoing, GRP, split_axis=0, concat_axis=0, tiled=True)
    own = lax.all_gather(mine, "z", axis=0, tiled=True)
    own = jnp.transpose(own, (1, 0, 2))
    other = lax.ppermute(own, "yl", [(0, 1), (1, 0)])

    wave = psi.astype(jnp.float32)
    norm = jnp.sum(jnp.sum(wave * wave, axis=(0, 1)).reshape(chunks, 1, LANES), axis=0)
    block = spg * part * chunks
    extra = 4
    stride = n_y * block + extra
    shape = (n_z, n_y, part, chunks, extra, stride)
    partials = partial_sums(groups, me, half.reshape(1), norm, own, other, left_ops[:, 0], incoming, shape)

    summed = lax.psum_scatter(partials, "z", scatter_dimension=0, tiled=True)
    summed = lax.optimization_barrier(summed)
    kept = lax.dynamic_slice_in_dim(summed, half * block, block, 0)
    given = lax.dynamic_slice_in_dim(summed, (1 - half) * block, block, 0)
    taken = lax.ppermute(given, "yl", [(0, 1), (1, 0)])
    scalars = summed[n_y * block : n_y * block + 2].reshape(1, 2, LANES)
    spread = ("yh", "x", "c", "yl")
    copies = jnp.broadcast_to(scalars, (lax.axis_size(spread), 2, LANES))
    copies = lax.all_to_all(copies, spread, split_axis=0, concat_axis=0, tiled=True)
    both = jnp.sum(copies, axis=(0, 2))
    theta = both[0] / both[1]
    sigma = (kept + taken).reshape(spg, chunks, part, LANES).transpose(0, 2, 1, 3).reshape(spg, part, cols)
    gap = precond_diag - theta
    correction = (sigma - theta * wave) * gap / (gap * gap + 1.0)
    return (sigma, correction)


def solution(mesh):
    split = Mesh(mesh.devices.reshape(2, 4, 2, 2, 16), GRP + OPS)
    return jax.shard_map(
        step,
        mesh=split,
        in_specs=(
            P(GRP, OPS, None),
            P(GRP, OPS, None, None),
            P(GRP, OPS, None, None),
            P(),
            P(),
            P(GRP, OPS, None),
        ),
        out_specs=(P(GRP, OPS, None), P(GRP, OPS, None)),
        check_vma=False,
    )
```

```python
import jax
import jax.numpy as jnp
from jax import lax
from jax.experimental import pallas as pl
from jax.experimental.pallas import tpu as pltpu
from jax.sharding import Mesh
from jax.sharding import PartitionSpec as P

GRP = ("yh", "x", "c")
COLUMN = ("zh", "zl")
OPS = ("yl",) + COLUMN
LANES = 128


def pick_kernel(groups_ref, slots_ref, me_ref, right_ref, out_ref, held_ref, in_sems, out_sems):
    spg, n_groups = held_ref.shape[0], out_ref.shape[0]
    loads = [pltpu.make_async_copy(right_ref.at[j], held_ref.at[j], in_sems.at[j]) for j in range(spg)]
    for load in loads:
        load.start()
    slots = []
    for g in range(n_groups):
        slot = jnp.int32(0)
        for j in range(spg):
            slot = jnp.where(groups_ref[g * spg + j] == me_ref[0], slots_ref[g * spg + j], slot)
        slots.append(slot)
    for load in loads:
        load.wait()
    stores = [pltpu.make_async_copy(held_ref.at[slots[g]], out_ref.at[g], out_sems.at[g]) for g in range(n_groups)]
    for store in stores:
        store.start()
    for store in stores:
        store.wait()


def outgoing_blocks(groups, slots, me, rights, n_groups):
    spg, rows, cols = rights.shape
    scalars = pl.BlockSpec(memory_space=pltpu.SMEM)
    return pl.pallas_call(
        pick_kernel,
        in_specs=[scalars, scalars, scalars, pl.BlockSpec(memory_space=pl.ANY)],
        out_specs=pl.BlockSpec(memory_space=pl.ANY),
        out_shape=jax.ShapeDtypeStruct((n_groups, rows, cols), rights.dtype),
        scratch_shapes=[
            pltpu.VMEM((spg, rows, cols), rights.dtype),
            pltpu.SemaphoreType.DMA((spg,)),
            pltpu.SemaphoreType.DMA((n_groups,)),
        ],
        name="pick",
    )(groups, slots, me, rights)


def sigma_kernel(shape, groups_ref, me_ref, place_ref, norm_ref, own_ref, other_ref, left_ref, right_ref, out_ref, stage_ref, rows_ref, psi_ref, image_ref, part_ref, corr_ref):
    n_z, n_y, part, chunks, extra, stride, spg = shape
    step_id = pl.program_id(0)
    half = n_z * part
    now, before = lax.rem(step_id, 2), lax.rem(step_id + 1, 2)
    sector = jnp.maximum(step_id - 1, 0)

    total = jnp.dot(left_ref[0], image_ref[before], preferred_element_type=jnp.float32)

    for source, held_ref in enumerate((own_ref, other_ref)):
        low = place_ref[1] if source == 0 else 1 - place_ref[1]
        for c in range(chunks):
            stage_ref[source, c] = held_ref[0, :, c * LANES : (c + 1) * LANES].astype(jnp.float32)
        for high in range(n_z // 2):
            for side in range(n_y):
                y = place_ref[0] if side == 0 else 1 - place_ref[0]
                start = y * half + (2 * high + low) * part
                for c in range(chunks):
                    rows_ref[c, pl.ds(start, part), :] = stage_ref[source, c, pl.ds((high * n_y + side) * part, part), :]
    for c in range(chunks):
        psi_ref[now, :, c * LANES : (c + 1) * LANES] = rows_ref[c].astype(jnp.bfloat16)
    image = lax.dot_general(psi_ref[now], right_ref[0], (((1,), (1,)), ((), ())), preferred_element_type=jnp.float32)
    image_ref[now] = image.astype(jnp.bfloat16)

    weighted = psi_ref[before].astype(jnp.float32) * total
    folded = jnp.sum(weighted.reshape(-1, 8, weighted.shape[1]), axis=0)
    corr = sum(folded[:, c * LANES : (c + 1) * LANES] for c in range(chunks))
    first = step_id == 1
    corr_ref[...] = jnp.where(first, corr, corr_ref[...] + corr)

    for c in range(chunks):
        part_ref[c] = total[:, c * LANES : (c + 1) * LANES]
    width = chunks * part
    block = spg * width
    for y in range(n_y):
        for z in range(n_z):
            for c in range(chunks):
                rows = part_ref[c, pl.ds(y * half + z * part, part), :]
                out_ref[pl.ds(z * stride + y * block + c * part + sector * width, part), :] = rows

    @pl.when(step_id == spg)
    def _():
        top = jnp.sum(corr_ref[...], axis=0, keepdims=True)
        below = jnp.zeros((extra - 2, LANES), jnp.float32)
        tail = jnp.concatenate([top, norm_ref[...], below], axis=0)
        for z in range(n_z):
            out_ref[pl.ds((z + 1) * stride - extra, extra), :] = tail


def partial_sums(groups, me, place, norm, own, other, lefts, incoming, shape):
    spg, rows, cols = lefts.shape
    n_z, _, _, chunks, _, stride = shape

    def kernel(*refs):
        sigma_kernel(shape + (spg,), *refs)

    def owner(j, groups_ref, me_ref, place_ref):
        return groups_ref[me_ref[0] * spg + jnp.minimum(j, spg - 1)], 0, 0

    half_rows = pl.BlockSpec((1, rows // 2, cols), lambda j, *_: (jnp.minimum(j, spg - 1), 0, 0))
    return pl.pallas_call(
        kernel,
        grid_spec=pltpu.PrefetchScalarGridSpec(
            num_scalar_prefetch=3,
            grid=(spg + 1,),
            in_specs=[
                pl.BlockSpec((1, LANES), lambda j, *_: (0, 0)),
                half_rows,
                half_rows,
                pl.BlockSpec((1, rows, cols), lambda j, *_: (jnp.maximum(j - 1, 0), 0, 0)),
                pl.BlockSpec((1, rows, cols), owner),
            ],
            out_specs=pl.BlockSpec((n_z * stride, LANES), lambda j, *_: (0, 0)),
            scratch_shapes=[
                pltpu.VMEM((2, chunks, rows // 2, LANES), jnp.float32),
                pltpu.VMEM((chunks, rows, LANES), jnp.float32),
                pltpu.VMEM((2, rows, cols), jnp.bfloat16),
                pltpu.VMEM((2, rows, cols), jnp.bfloat16),
                pltpu.VMEM((chunks, rows, LANES), jnp.float32),
                pltpu.VMEM((8, LANES), jnp.float32),
            ],
        ),
        out_shape=jax.ShapeDtypeStruct((n_z * stride, LANES), jnp.float32),
        name="partial",
    )(groups, me, place, norm, own, other, lefts, incoming)


def step(psi, left_ops, right_ops, right_group, right_slot, precond_diag):
    n_groups, n_z, n_y = lax.axis_size(GRP), lax.axis_size(COLUMN), lax.axis_size("yl")
    spg, part, cols = psi.shape
    chunks = cols // LANES
    me = lax.axis_index(GRP).astype(jnp.int32).reshape(1)
    half = lax.axis_index("yl").astype(jnp.int32)
    groups = right_group.reshape(-1)

    swap = [(0, 1), (1, 0)]
    mine = jnp.transpose(psi, (1, 0, 2))
    theirs = lax.ppermute(mine, "yl", swap)
    outgoing = outgoing_blocks(groups, right_slot, me, right_ops[:, 0], n_groups)
    incoming = lax.all_to_all(outgoing, GRP, split_axis=0, concat_axis=0, tiled=True)
    own = lax.all_gather(jnp.concatenate([mine, theirs], axis=0), "zh", axis=0, tiled=True)
    own = jnp.transpose(own, (1, 0, 2))
    other = lax.ppermute(own, "zl", swap)

    wave = psi.astype(jnp.float32)
    norm = jnp.sum(jnp.sum(wave * wave, axis=(0, 1)).reshape(chunks, 1, LANES), axis=0)
    block = spg * part * chunks
    extra = 4
    stride = n_y * block + extra
    shape = (n_z, n_y, part, chunks, extra, stride)
    place = jnp.stack([half, lax.axis_index("zl").astype(jnp.int32)])
    partials = partial_sums(groups, me, place, norm, own, other, left_ops[:, 0], incoming, shape)

    summed = lax.psum_scatter(partials, COLUMN, scatter_dimension=0, tiled=True)
    summed = lax.optimization_barrier(summed)
    kept = lax.dynamic_slice_in_dim(summed, half * block, block, 0)
    given = lax.dynamic_slice_in_dim(summed, (1 - half) * block, block, 0)
    taken = lax.ppermute(given, "yl", swap)
    scalars = summed[n_y * block : n_y * block + 2].reshape(1, 2, LANES)
    spread = ("yh", "x", "c", "yl")
    copies = jnp.broadcast_to(scalars, (lax.axis_size(spread), 2, LANES))
    copies = lax.all_to_all(copies, spread, split_axis=0, concat_axis=0, tiled=True)
    both = jnp.sum(copies, axis=(0, 2))
    theta = both[0] / both[1]
    sigma = (kept + taken).reshape(spg, chunks, part, LANES).transpose(0, 2, 1, 3).reshape(spg, part, cols)
    gap = precond_diag - theta
    correction = (sigma - theta * wave) * gap / (gap * gap + 1.0)
    return (sigma, correction)


def solution(mesh):
    split = Mesh(mesh.devices.reshape(2, 4, 2, 2, 8, 2), GRP + OPS)
    return jax.shard_map(
        step,
        mesh=split,
        in_specs=(
            P(GRP, OPS, None),
            P(GRP, OPS, None, None),
            P(GRP, OPS, None, None),
            P(),
            P(),
            P(GRP, OPS, None),
        ),
        out_specs=(P(GRP, OPS, None), P(GRP, OPS, None)),
        check_vma=False,
    )
```

```python
import jax
import jax.numpy as jnp
from jax import lax
from jax.experimental import pallas as pl
from jax.experimental.pallas import tpu as pltpu
from jax.experimental.layout import Layout, with_layout_constraint
from jax.sharding import Mesh
from jax.sharding import PartitionSpec as P

GRP = ("yh", "x", "c")
COLUMN = ("zh", "zl")
OPS = ("yl",) + COLUMN
LANES = 128


def pick_kernel(groups_ref, slots_ref, me_ref, right_ref, out_ref, held_ref, in_sems, out_sems):
    spg, n_groups = held_ref.shape[0], out_ref.shape[0]
    loads = [pltpu.make_async_copy(right_ref.at[j], held_ref.at[j], in_sems.at[j]) for j in range(spg)]
    for load in loads:
        load.start()
    slots = []
    for g in range(n_groups):
        slot = jnp.int32(0)
        for j in range(spg):
            slot = jnp.where(groups_ref[g * spg + j] == me_ref[0], slots_ref[g * spg + j], slot)
        slots.append(slot)
    for load in loads:
        load.wait()
    stores = [pltpu.make_async_copy(held_ref.at[slots[g]], out_ref.at[g], out_sems.at[g]) for g in range(n_groups)]
    for store in stores:
        store.start()
    for store in stores:
        store.wait()


def outgoing_blocks(groups, slots, me, rights, n_groups):
    spg, rows, cols = rights.shape
    scalars = pl.BlockSpec(memory_space=pltpu.SMEM)
    return pl.pallas_call(
        pick_kernel,
        in_specs=[scalars, scalars, scalars, pl.BlockSpec(memory_space=pl.ANY)],
        out_specs=pl.BlockSpec(memory_space=pl.ANY),
        out_shape=jax.ShapeDtypeStruct((n_groups, rows, cols), rights.dtype),
        scratch_shapes=[
            pltpu.VMEM((spg, rows, cols), rights.dtype),
            pltpu.SemaphoreType.DMA((spg,)),
            pltpu.SemaphoreType.DMA((n_groups,)),
        ],
        name="pick",
    )(groups, slots, me, rights)


def order_kernel(shape, place_ref, own_ref, below_ref, above_ref, out_ref, stage_ref, rows_ref):
    n_z, n_y, part, chunks = shape
    half = n_z * part
    cut = below_ref.shape[1]
    for c in range(chunks):
        lanes = pl.ds(c * LANES, LANES)
        stage_ref[0, c] = own_ref[0, :, lanes].astype(jnp.float32)
        stage_ref[1, c, :cut, :] = below_ref[0, :, lanes].astype(jnp.float32)
        stage_ref[1, c, cut:, :] = above_ref[0, :, lanes].astype(jnp.float32)
    for source in range(2):
        low = place_ref[1] if source == 0 else 1 - place_ref[1]
        for high in range(n_z // 2):
            for side in range(n_y):
                y = place_ref[0] if side == 0 else 1 - place_ref[0]
                start = y * half + (2 * high + low) * part
                for c in range(chunks):
                    rows_ref[c, pl.ds(start, part), :] = stage_ref[source, c, pl.ds((high * n_y + side) * part, part), :]
    for c in range(chunks):
        out_ref[0, :, c * LANES : (c + 1) * LANES] = rows_ref[c].astype(jnp.bfloat16)


def ordered_rows(place, own, below, above, shape):
    spg, half, cols = own.shape
    chunks = cols // LANES

    def kernel(*refs):
        order_kernel(shape, *refs)

    def of_sector(rows):
        return pl.BlockSpec((1, rows, cols), lambda j, *_: (j, 0, 0))

    return pl.pallas_call(
        kernel,
        grid_spec=pltpu.PrefetchScalarGridSpec(
            num_scalar_prefetch=1,
            grid=(spg,),
            in_specs=[of_sector(half), of_sector(below.shape[1]), of_sector(above.shape[1])],
            out_specs=of_sector(2 * half),
            scratch_shapes=[
                pltpu.VMEM((2, chunks, half, LANES), jnp.float32),
                pltpu.VMEM((chunks, 2 * half, LANES), jnp.float32),
            ],
        ),
        out_shape=jax.ShapeDtypeStruct((spg, 2 * half, cols), own.dtype),
        name="order",
    )(place, own, below, above)


def sigma_kernel(shape, groups_ref, me_ref, norm_ref, rows_ref, left_ref, right_ref, out_ref, psi_ref, image_ref, part_ref, corr_ref):
    n_z, n_y, part, chunks, extra, stride, spg = shape
    step_id = pl.program_id(0)
    half = n_z * part
    now, before = lax.rem(step_id, 2), lax.rem(step_id + 1, 2)
    sector = jnp.maximum(step_id - 1, 0)

    def project():
        psi_ref[now] = rows_ref[0]
        image = lax.dot_general(rows_ref[0], right_ref[0], (((1,), (1,)), ((), ())), preferred_element_type=jnp.float32)
        image_ref[now] = image.astype(jnp.bfloat16)

    def apply_left():
        return jnp.dot(left_ref[0], image_ref[before], preferred_element_type=jnp.float32)

    def spread(total):
        weighted = psi_ref[before].astype(jnp.float32) * total
        folded = jnp.sum(weighted.reshape(-1, 8, weighted.shape[1]), axis=0)
        corr = sum(folded[:, c * LANES : (c + 1) * LANES] for c in range(chunks))
        first = step_id == 1
        corr_ref[...] = jnp.where(first, corr, corr_ref[...] + corr)
        for c in range(chunks):
            part_ref[c] = total[:, c * LANES : (c + 1) * LANES]
        width = chunks * part
        block = spg * width
        for y in range(n_y):
            for z in range(n_z):
                for c in range(chunks):
                    rows = part_ref[c, pl.ds(y * half + z * part, part), :]
                    out_ref[pl.ds(z * stride + y * block + c * part + sector * width, part), :] = rows

    @pl.when(step_id == 0)
    def _():
        project()

    @pl.when((step_id > 0) & (step_id < spg))
    def _():
        total = apply_left()
        project()
        spread(total)

    @pl.when(step_id == spg)
    def _():
        spread(apply_left())

    @pl.when(step_id == spg)
    def _():
        top = jnp.sum(corr_ref[...], axis=0, keepdims=True)
        below = jnp.zeros((extra - 2, LANES), jnp.float32)
        tail = jnp.concatenate([top, norm_ref[...], below], axis=0)
        for z in range(n_z):
            out_ref[pl.ds((z + 1) * stride - extra, extra), :] = tail


def partial_sums(groups, me, norm, whole, lefts, incoming, shape):
    spg, rows, cols = lefts.shape
    n_z, _, _, chunks, _, stride = shape

    def kernel(*refs):
        sigma_kernel(shape + (spg,), *refs)

    def owner(j, groups_ref, me_ref):
        return groups_ref[me_ref[0] * spg + jnp.minimum(j, spg - 1)], 0, 0

    return pl.pallas_call(
        kernel,
        grid_spec=pltpu.PrefetchScalarGridSpec(
            num_scalar_prefetch=2,
            grid=(spg + 1,),
            in_specs=[
                pl.BlockSpec((1, LANES), lambda j, *_: (0, 0)),
                pl.BlockSpec((1, rows, cols), lambda j, *_: (jnp.minimum(j, spg - 1), 0, 0)),
                pl.BlockSpec((1, rows, cols), lambda j, *_: (jnp.maximum(j - 1, 0), 0, 0)),
                pl.BlockSpec((1, rows, cols), owner),
            ],
            out_specs=pl.BlockSpec((n_z * stride, LANES), lambda j, *_: (0, 0)),
            scratch_shapes=[
                pltpu.VMEM((2, rows, cols), jnp.bfloat16),
                pltpu.VMEM((2, rows, cols), jnp.bfloat16),
                pltpu.VMEM((chunks, rows, LANES), jnp.float32),
                pltpu.VMEM((8, LANES), jnp.float32),
            ],
        ),
        out_shape=jax.ShapeDtypeStruct((n_z * stride, LANES), jnp.float32),
        name="partial",
    )(groups, me, norm, whole, lefts, incoming)


def step(psi, left_ops, right_ops, right_group, right_slot, precond_diag):
    n_groups, n_z, n_y = lax.axis_size(GRP), lax.axis_size(COLUMN), lax.axis_size("yl")
    spg, part, cols = psi.shape
    chunks = cols // LANES
    me = lax.axis_index(GRP).astype(jnp.int32).reshape(1)
    half = lax.axis_index("yl").astype(jnp.int32)
    groups = right_group.reshape(-1)

    swap = [(0, 1), (1, 0)]
    mine = jnp.transpose(psi, (1, 0, 2))
    theirs = lax.ppermute(with_layout_constraint(mine, Layout(major_to_minor=(0, 1, 2))), "yl", swap)
    theirs = with_layout_constraint(theirs, Layout(major_to_minor=(0, 1, 2)))
    outgoing = outgoing_blocks(groups, right_slot, me, right_ops[:, 0], n_groups)
    incoming = lax.all_to_all(outgoing, GRP, split_axis=0, concat_axis=0, tiled=True)
    own = lax.all_gather(jnp.concatenate([mine, theirs], axis=0), "zh", axis=0, tiled=True)
    own = jnp.transpose(own, (1, 0, 2))
    cut = own.shape[1] // 2
    around = [(i, (i + 1) % n_z) for i in range(n_z)]
    below = lax.ppermute(own[:, :cut], COLUMN, around)
    above = lax.ppermute(own[:, cut:], COLUMN, [(b, a) for a, b in around])

    wave = psi.astype(jnp.float32)
    norm = jnp.sum(jnp.sum(wave * wave, axis=(0, 1)).reshape(chunks, 1, LANES), axis=0)
    block = spg * part * chunks
    extra = 4
    stride = n_y * block + extra
    shape = (n_z, n_y, part, chunks, extra, stride)
    place = jnp.stack([half, lax.axis_index("zl").astype(jnp.int32)])
    whole = ordered_rows(place, own, below, above, (n_z, n_y, part, chunks))
    partials = partial_sums(groups, me, norm, whole, left_ops[:, 0], incoming, shape)

    summed = lax.psum_scatter(partials, COLUMN, scatter_dimension=0, tiled=True)
    summed = lax.optimization_barrier(summed)
    kept = lax.dynamic_slice_in_dim(summed, half * block, block, 0)
    given = lax.dynamic_slice_in_dim(summed, (1 - half) * block, block, 0)
    taken = lax.ppermute(given, "yl", swap)
    scalars = summed[n_y * block : n_y * block + 2].reshape(1, 2, LANES)
    spread = ("yh", "x", "c", "yl")
    copies = jnp.broadcast_to(scalars, (lax.axis_size(spread), 2, LANES))
    copies = lax.all_to_all(copies, spread, split_axis=0, concat_axis=0, tiled=True)
    both = jnp.sum(copies, axis=(0, 2))
    theta = both[0] / both[1]
    sigma = (kept + taken).reshape(spg, chunks, part, LANES).transpose(0, 2, 1, 3).reshape(spg, part, cols)
    gap = precond_diag - theta
    correction = (sigma - theta * wave) * gap / (gap * gap + 1.0)
    return (sigma, correction)


def solution(mesh):
    split = Mesh(mesh.devices.reshape(2, 4, 2, 2, 8, 2), GRP + OPS)
    return jax.shard_map(
        step,
        mesh=split,
        in_specs=(
            P(GRP, OPS, None),
            P(GRP, OPS, None, None),
            P(GRP, OPS, None, None),
            P(),
            P(),
            P(GRP, OPS, None),
        ),
        out_specs=(P(GRP, OPS, None), P(GRP, OPS, None)),
        check_vma=False,
    )
```
